256 devices in a mesh: wedge: 4 (over y), box: 64 (over x, z, core).
Axes of the slice: x: 4, y: 4, z: 8, core: 2. Of those that a mesh axis runs over, the one named last changes fastest.
Arguments:
- densities: bfloat16 [2048, 4, 128], P('box', 'wedge'), may hold values from -6 to 6
- up_ops: bfloat16 [96, 128, 128], replicated, may hold values from -0.5 to 0.5
- trans_ops: bfloat16 [16, 128, 128], replicated, may hold values from -0.125 to 0.125
- down_ops: bfloat16 [96, 128, 128], replicated, may hold values from -0.0546875 to 0.0546875
- read_table: int32 [64, 128], P('box'), may hold values from 0 to 2047, as said below
- interaction: int32 [2048, 96, 16], P('box', 'wedge'), may hold values from 0 to 127
Outputs:
- potentials: bfloat16 [2048, 4, 128], P('box', 'wedge')
The draws below stay inside these ranges and needn't reach their ends.
Inputs may be any that keep to these rules, and one draw needn't show every extreme that they name: `read_table`: row r holds, for each box group o in order, 2 distinct boxes owned by box group o, numbered o * 32 to o * 32 + 31. interaction[b, w, k] indexes row b // 32 of read_table.
All inputs are finite; a program needn't handle non-finite values.
Results may differ from the reference program's by a relative error of at most 0.0057.
Values may be sent and summed in bfloat16 or wider, within the bound.
No kernel may reach another device: no remote copies, remote signals or barrier semaphores. Data moves between devices by JAX's collectives and lax.ppermute only.
A program may use at most 128 MiB of HBM per device.

```python
import math
import jax
import jax.numpy as jnp
from jax import lax

W = 96
C = 128
P_SIZE = 128
F = 4
LIST = 16
BOX_DEV = 32
BOXES = 2048
READS = 128
CAP = 2
N_BOX = 64


def draw_read_table(key, part):
    scores = jax.random.randint(key, (N_BOX, N_BOX, BOX_DEV), 0, 1 << 20) * BOX_DEV
    scores = scores + jnp.arange(BOX_DEV, dtype=jnp.int32)
    ordered = jnp.argsort(scores, axis=-1)[:, :, :CAP].astype(jnp.int32)
    owners = jnp.arange(N_BOX, dtype=jnp.int32)[None, :, None] * BOX_DEV
    return (ordered + owners).reshape(N_BOX, READS).astype(jnp.int32)


def place_ends(result, own_key, least, high):
    longest = result.shape.index(max(result.shape))
    spots = []
    for shift in (0, 1):
        where = [jax.random.randint(jax.random.fold_in(own_key, axis), (), 0, length) for axis, length in enumerate(result.shape)]
        where[longest] = (where[longest] + shift) % result.shape[longest]
        spots.append(tuple(where))
    return result.at[spots[0]].set(least).at[spots[1]].set(high)


def block_scale(key, extent, split, low, top_value):
    def one(position, shards_of):
        draws = jax.random.uniform(jax.random.fold_in(jax.random.fold_in(key, 6), position), (shards_of,), jnp.float32, low / len(split), top_value / len(split))
        return jnp.repeat(jnp.exp(draws), extent[position] // shards_of).reshape((-1,) + (1,) * (len(extent) - position - 1))

    loudness = one(*split[0])
    for cut in split[1:]:
        loudness = loudness * one(*cut)
    return loudness


def gaussian(own_key, dims, scale, limit, shards=(), kind=jnp.bfloat16):
    result = jax.random.normal(own_key, dims, jnp.float32) * scale
    if len(shards) > 0:
        result = block_scale(own_key, dims, shards, -0.22, 0.18) * result
    return jnp.clip(result, min=-limit, max=limit).astype(kind)


def setup_inputs(seed: int = 0) -> dict:
    key_of = jax.random.split(jax.random.key(seed), 7)
    return {
        "densities": gaussian(key_of[0], (BOXES, F, P_SIZE), 1.0, 6.0, ((0, 64), (1, 4))),
        "up_ops": gaussian(key_of[1], (W, C, P_SIZE), P_SIZE ** -0.5, 0.5),
        "trans_ops": gaussian(key_of[2], (LIST, C, C), (C * LIST) ** -0.5, 0.125),
        "down_ops": gaussian(key_of[3], (W, P_SIZE, C), (W * C) ** -0.5, 0.0546875),
        "read_table": draw_read_table(jax.random.fold_in(key_of[6], 71), 0),
        "interaction": place_ends(jax.random.randint(key_of[5], (BOXES, W, LIST), 0, READS), jax.random.fold_in(key_of[5], 1), 0, READS - 1).astype(jnp.int32),
    }


def reference(densities, up_ops, trans_ops, down_ops, read_table, interaction):
    group = (jnp.arange(BOXES) // BOX_DEV).astype(jnp.int32)
    source_all = read_table[group[:, None, None], interaction]
    dens_wide = densities.astype(jnp.float32)
    trans_wide = trans_ops.astype(jnp.float32)
    block = math.gcd(BOXES, 512)
    starts = jnp.arange(0, BOXES, block).astype(jnp.int32)

    def wedge_step(carry, wedge_at):
        up_here = lax.dynamic_index_in_dim(up_ops, wedge_at, 0, keepdims=False).astype(jnp.float32)
        down_here = lax.dynamic_index_in_dim(down_ops, wedge_at, 0, keepdims=False).astype(jnp.float32)
        equivalents = jnp.einsum("bfp,cp->bfc", dens_wide, up_here).astype(jnp.bfloat16)
        source_here = lax.dynamic_index_in_dim(source_all, wedge_at, 1, keepdims=False)

        def one_block(start):
            chosen = lax.dynamic_slice_in_dim(source_here, start, block, 0)
            picked = equivalents[chosen].astype(jnp.float32)
            return jnp.einsum("bkfc,kdc->bfd", picked, trans_wide).astype(jnp.bfloat16)

        local_here = lax.map(one_block, starts).reshape(BOXES, F, C)
        carry = carry + jnp.einsum("bfc,pc->bfp", local_here.astype(jnp.float32), down_here)
        return carry, None

    initial = jnp.zeros((BOXES, F, P_SIZE), jnp.float32)
    summed, _ = lax.scan(wedge_step, initial, jnp.arange(W).astype(jnp.int32))
    return summed.astype(jnp.bfloat16)
```

```python
import jax
import jax.numpy as jnp
from jax import lax
from jax.experimental import pallas as pl
from jax.experimental.pallas import tpu as pltpu
from jax.sharding import PartitionSpec as P

BF = jnp.bfloat16
F32 = jnp.float32
NT = (((1,), (1,)), ((), ()))
GROUP = 8


def columns_kernel(list_ref, out_ref):
    wedges, length, boxes = list_ref.shape
    flat = list_ref[...].astype(F32).reshape(wedges * length, boxes)
    out_ref[...] = flat.T.astype(BF)


def selector_kernel(columns_ref, target_ref, trans_ref, sel_ref, pick_ref, tcat_ref):
    step = pl.program_id(0)
    slots = target_ref.shape[1]
    boxes = columns_ref.shape[1]
    length = trans_ref.shape[0]
    group = sel_ref.shape[0]
    lane = lax.broadcasted_iota(jnp.int32, (boxes, slots), 1).astype(F32).astype(BF)
    cols = columns_ref[0]
    for w in range(group):
        for k in range(length):
            at = w * length + k
            hit = jnp.broadcast_to(cols[:, at : at + 1], (boxes, slots)) == lane
            sel_ref[w, (k // 2) * boxes : (k // 2 + 1) * boxes, (k % 2) * slots : (k % 2 + 1) * slots] = (
                jnp.where(hit, jnp.ones_like(lane), jnp.zeros_like(lane))
            )

    @pl.when(step == 0)
    def _():
        total = pick_ref.shape[1]
        wide = jnp.broadcast_to(target_ref[...].astype(F32), (slots, slots)).T
        for j in range(total // slots):
            number = lax.broadcasted_iota(jnp.int32, (slots, slots), 1).astype(F32) + float(j * slots)
            pick_ref[:, j * slots : (j + 1) * slots] = jnp.where(wide == number, 1.0, 0.0).astype(BF)
        c = trans_ref.shape[2]
        for k in range(length):
            tcat_ref[k * c : (k + 1) * c, :] = trans_ref[k].T


def main_kernel(near_ref, far_ref, pick_ref, sel_ref, up_ref, tcat_ref, down_ref, out_ref, dens, blocks, wide, acc):
    step = pl.program_id(0)
    group, c, p = up_ref.shape
    half = near_ref.shape[0]
    slots = pick_ref.shape[0]
    boxes = out_ref.shape[0]
    pairs = sel_ref.shape[1] // boxes

    @pl.when(step == 0)
    def _():
        picked = jnp.dot(pick_ref[:, :half], near_ref[...], preferred_element_type=F32)
        picked += jnp.dot(pick_ref[:, half:], far_ref[...], preferred_element_type=F32)
        dens[...] = picked.astype(BF)
        blocks[...] = jnp.zeros_like(blocks)
        acc[...] = jnp.zeros_like(acc)

    equivalents = lax.dot_general(
        dens[...], up_ref[...].reshape(group * c, p), NT, preferred_element_type=F32
    ).astype(BF)
    for w in range(group):
        one = equivalents[:, w * c : (w + 1) * c]
        blocks[w, :slots, :c] = one
        blocks[w, slots:, c:] = one
    for w in range(group):
        sources = jnp.dot(sel_ref[w], blocks[w], preferred_element_type=F32).astype(BF)
        for j in range(pairs):
            wide[w * boxes : (w + 1) * boxes, j * 2 * c : (j + 1) * 2 * c] = sources[j * boxes : (j + 1) * boxes]
    local = jnp.dot(wide[...], tcat_ref[...], preferred_element_type=F32).astype(BF)
    total = acc[...]
    for w in range(group):
        total += lax.dot_general(
            local[w * boxes : (w + 1) * boxes], down_ref[w], NT, preferred_element_type=F32
        )
    acc[...] = total

    @pl.when(step == pl.num_programs(0) - 1)
    def _():
        out_ref[...] = total.astype(BF)


def solution(mesh):
    x_chips, z_chips, cores = 4, 8, 2
    groups = [[(x * z_chips + z) * cores + c for x in range(x_chips) for z in range(z_chips)] for c in range(cores)]
    swap = [(i, i ^ 1) for i in range(x_chips * z_chips * cores)]

    def body(densities, up_ops, trans_ops, down_ops, read_table, interaction):
        boxes, _, p = densities.shape
        wedges, c, _ = up_ops.shape
        wedge_here, length = interaction.shape[1:]
        wedge_groups = wedges // wedge_here
        slots = read_table.shape[1]
        chips = len(groups[0])
        half = chips * boxes

        own = densities.reshape(boxes, p)
        copies = jnp.broadcast_to(own[None], (chips, boxes, p))
        near = lax.all_to_all(copies, "box", 0, 0, axis_index_groups=groups).reshape(half, p)

        lists = interaction.transpose(1, 2, 0)
        columns = pl.pallas_call(
            columns_kernel,
            out_shape=jax.ShapeDtypeStruct((boxes, wedge_here * length), BF),
            name="columns",
        )(lists)
        spread = jnp.broadcast_to(columns[None], (wedge_groups,) + columns.shape)
        spread = lax.all_to_all(spread, "wedge", 0, 0)

        core = lax.axis_index("box") % cores
        owner = read_table // boxes
        target = (owner % cores != core) * half + owner // cores * boxes + read_table % boxes

        steps = wedges // GROUP
        per = steps // wedge_groups
        sel, pick, tcat = pl.pallas_call(
            selector_kernel,
            grid=(steps,),
            in_specs=[
                pl.BlockSpec((1, boxes, GROUP * length), lambda i: (i // per, 0, i % per)),
                pl.BlockSpec((1, slots), lambda i: (0, 0)),
                pl.BlockSpec((length, c, c), lambda i: (0, 0, 0)),
            ],
            out_specs=[
                pl.BlockSpec((GROUP, length // 2 * boxes, 2 * slots), lambda i: (i, 0, 0)),
                pl.BlockSpec((slots, 2 * half), lambda i: (0, 0)),
                pl.BlockSpec((length * c, c), lambda i: (0, 0)),
            ],
            out_shape=[
                jax.ShapeDtypeStruct((wedges, length // 2 * boxes, 2 * slots), BF),
                jax.ShapeDtypeStruct((slots, 2 * half), BF),
                jax.ShapeDtypeStruct((length * c, c), BF),
            ],
            compiler_params=pltpu.CompilerParams(vmem_limit_bytes=16 << 20),
            name="selectors",
        )(spread, target, trans_ops)

        far = lax.ppermute(near, "box", swap)

        out = pl.pallas_call(
            main_kernel,
            grid=(steps,),
            in_specs=[
                pl.BlockSpec((half, p), lambda i: (0, 0)),
                pl.BlockSpec((half, p), lambda i: (0, 0)),
                pl.BlockSpec((slots, 2 * half), lambda i: (0, 0)),
                pl.BlockSpec((GROUP, length // 2 * boxes, 2 * slots), lambda i: (i, 0, 0)),
                pl.BlockSpec((GROUP, c, p), lambda i: (i, 0, 0)),
                pl.BlockSpec((length * c, c), lambda i: (0, 0)),
                pl.BlockSpec((GROUP, p, c), lambda i: (i, 0, 0)),
            ],
            out_specs=pl.BlockSpec((boxes, p), lambda i: (0, 0)),
            out_shape=jax.ShapeDtypeStruct((boxes, p), BF),
            scratch_shapes=[
                pltpu.VMEM((slots, p), BF),
                pltpu.VMEM((GROUP, 2 * slots, 2 * c), BF),
                pltpu.VMEM((GROUP * boxes, length * c), BF),
                pltpu.VMEM((boxes, p), F32),
            ],
            compiler_params=pltpu.CompilerParams(vmem_limit_bytes=24 << 20),
            name="main",
        )(near, far, pick, sel, up_ops, tcat, down_ops)
        return out.reshape(boxes, 1, p)

    in_specs = (P("box", "wedge", None), P(), P(), P(), P("box", None), P("box", "wedge", None))
    out_specs = P("box", "wedge", None)
    return jax.shard_map(body, mesh=mesh, in_specs=in_specs, out_specs=out_specs, check_vma=False)
```

```python
import functools

import jax
import jax.numpy as jnp
from jax import lax
from jax.experimental import pallas as pl
from jax.experimental.pallas import tpu as pltpu
from jax.sharding import PartitionSpec as P


BF = jnp.bfloat16
F32 = jnp.float32
NT = (((1,), (1,)), ((), ()))
GROUP = 8
VMEM = pl.BlockSpec(memory_space=pltpu.VMEM)
SMEM = pl.BlockSpec(memory_space=pltpu.SMEM)
HBM = pl.BlockSpec(memory_space=pltpu.HBM)


def pack_kernel(list_ref, out_ref):
    length, boxes = list_ref.shape[1:]
    for k in range(length):
        out_ref[:, k * boxes : (k + 1) * boxes] = list_ref[:, k, :].astype(F32).astype(BF)


def table_kernel(place_ref, table_ref, trans_ref, *refs):
    list_refs, (pick_ref, tcat_ref, lists_ref) = refs[:-3], refs[-3:]
    here = list_refs[0].shape[0]
    for n, ref in enumerate(list_refs):
        lists_ref[n * here : (n + 1) * here, :] = ref[...].astype(F32)
    slots = table_ref.shape[1]
    length, c, _ = trans_ref.shape
    half = pick_ref.shape[1] // 2
    table = table_ref[...]
    owner = table >> 5
    other = (owner & 1) != place_ref[0]
    target = jnp.where(other, half, 0) + ((owner >> 1) << 5) + (table & 31)
    spread = jnp.broadcast_to(target.astype(F32), (slots, slots)).T
    number = lax.broadcasted_iota(jnp.int32, (slots, slots), 1).astype(F32)
    for j in range(2 * half // slots):
        pick_ref[:, j * slots : (j + 1) * slots] = jnp.where(spread == number + float(j * slots), 1.0, 0.0).astype(BF)
    for k in range(length):
        at = (k % (length // 2)) * 2 * c + k // (length // 2) * c
        tcat_ref[at : at + c, :] = trans_ref[k].T


def main_kernel(
    pieces, place_ref, near_ref, far_ref, pick_ref, tcat_ref, lists, up_hbm, down_hbm, out_ref,
    dens, blocks, sel, wide, up, down, sems,
):
    wedges, c, p = up.shape
    half = near_ref.shape[0]
    slots = pick_ref.shape[0]
    boxes = out_ref.shape[0]
    pairs = sel.shape[2] // boxes
    here = wedges // pieces
    steps = wedges // GROUP
    per = here // GROUP

    def fetch(hbm, held, kind, i):
        group = lax.rem(place_ref[1] + pieces - i // per, pieces)
        source = pl.ds(pl.multiple_of(group * here + i % per * GROUP, GROUP), GROUP)
        return pltpu.make_async_copy(hbm.at[source], held.at[pl.ds(i * GROUP, GROUP)], sems.at[kind, i])

    def fetch_up(i):
        return fetch(up_hbm, up, 0, i)

    def fetch_down(i):
        return fetch(down_hbm, down, 1, i)

    for i in range(steps):
        fetch_up(i).start()
        fetch_down(i).start()

    blocks[...] = jnp.zeros_like(blocks)
    number = lax.broadcasted_iota(jnp.int32, (slots, slots), 0).astype(F32)
    chunks = lists.shape[1] // slots

    def rows_of(i):
        return lists[pl.ds(pl.multiple_of(i * GROUP, GROUP), GROUP), :]

    def select(rows, slot, w):
        for j in range(chunks):
            row = jnp.broadcast_to(rows[w : w + 1, j * slots : (j + 1) * slots], (slots, slots))
            hit = jnp.where(row == number, 1.0, 0.0).astype(BF)
            top, left = j % (chunks // 2) * slots, j // (chunks // 2) * slots
            sel[slot, w, top : top + slots, left : left + slots] = hit.T

    def equivalents(i, slot):
        maps = up[pl.ds(pl.multiple_of(i * GROUP, GROUP), GROUP)].reshape(GROUP * c, p)
        value = lax.dot_general(dens[...], maps, NT, preferred_element_type=F32).astype(BF)
        for w in range(GROUP):
            one = value[:, w * c : (w + 1) * c]
            blocks[slot, w, :slots, :c] = one
            blocks[slot, w, slots:, c:] = one

    rows = rows_of(0)
    for w in range(GROUP):
        select(rows, 0, w)
    picked = jnp.dot(pick_ref[:, :half], near_ref[...], preferred_element_type=F32)
    picked += jnp.dot(pick_ref[:, half:], far_ref[...], preferred_element_type=F32)
    dens[...] = picked.astype(BF)
    fetch_up(0).wait()
    equivalents(0, 0)

    def step(b, total):
        first = b * 2
        fetch_up(first + 1).wait()
        fetch_down(first).wait()
        fetch_down(first + 1).wait()

        @pl.when(b < steps // 2 - 1)
        def _():
            fetch_up(first + 2).wait()

        for h in (0, 1):
            now = first + h
            later = lax.rem(now + 1, steps)
            rows = rows_of(later)
            for w in range(GROUP):
                sources = jnp.dot(sel[h, w], blocks[h, w], preferred_element_type=F32).astype(BF)
                for j in range(pairs):
                    wide[h, w * boxes : (w + 1) * boxes, j * 2 * c : (j + 1) * 2 * c] = (
                        sources[j * boxes : (j + 1) * boxes]
                    )
                select(rows, 1 - h, w)
            equivalents(later, 1 - h)
            local = jnp.dot(wide[h], tcat_ref[...], preferred_element_type=F32).astype(BF)
            flat = jnp.concatenate([local[w * boxes : (w + 1) * boxes] for w in range(GROUP)], 1)
            maps = jnp.concatenate([down[now * GROUP + w] for w in range(GROUP)], 1)
            total = total + lax.dot_general(flat, maps, NT, preferred_element_type=F32)
        return total

    total = lax.fori_loop(0, steps // 2, step, jnp.zeros((boxes, p), F32))
    out_ref[...] = total.astype(BF)


def solution(mesh):
    x_chips, z_chips, cores = 4, 8, 2
    groups = [[(x * z_chips + z) * cores + c for x in range(x_chips) for z in range(z_chips)] for c in range(cores)]
    swap = [(i, i ^ 1) for i in range(x_chips * z_chips * cores)]

    def parts(densities, up_ops, trans_ops, down_ops, read_table, interaction):
        boxes, _, p = densities.shape
        wedges, c, _ = up_ops.shape
        wedge_here, length = interaction.shape[1:]
        wedge_groups = wedges // wedge_here
        slots = read_table.shape[1]
        chips = len(groups[0])
        half = chips * boxes
        width = length * boxes

        copies = jnp.broadcast_to(densities.reshape(1, boxes, p), (chips, boxes, p))
        near = lax.all_to_all(copies, "box", 0, 0, axis_index_groups=groups)
        near = near.reshape(half, p)

        lists = pl.pallas_call(
            pack_kernel,
            in_specs=[VMEM],
            out_specs=VMEM,
            out_shape=jax.ShapeDtypeStruct((wedge_here, width), BF),
            compiler_params=pltpu.CompilerParams(vmem_limit_bytes=4 << 20),
            name="pack",
        )(interaction.transpose(1, 2, 0))
        spread = [lists]
        for j in range(1, wedge_groups):
            spread.append(lax.ppermute(lists, "wedge", [(i, (i + j) % wedge_groups) for i in range(wedge_groups)]))
        place = jnp.stack([lax.axis_index("box") % cores, lax.axis_index("wedge")])

        pick, tcat, lists = pl.pallas_call(
            table_kernel,
            in_specs=[SMEM] + [VMEM] * (2 + wedge_groups),
            out_specs=[VMEM] * 3,
            out_shape=[
                jax.ShapeDtypeStruct((slots, 2 * half), BF),
                jax.ShapeDtypeStruct((length * c, c), BF),
                jax.ShapeDtypeStruct((wedges, width), F32),
            ],
            compiler_params=pltpu.CompilerParams(vmem_limit_bytes=4 << 20),
            name="tables",
        )(place, read_table, trans_ops, *spread)

        far = lax.ppermute(near, "box", swap)

        out = pl.pallas_call(
            functools.partial(main_kernel, wedge_groups),
            in_specs=[SMEM] + [VMEM] * 5 + [HBM, HBM],
            out_specs=VMEM,
            out_shape=jax.ShapeDtypeStruct((boxes, p), BF),
            scratch_shapes=[
                pltpu.VMEM((slots, p), BF),
                pltpu.VMEM((2, GROUP, 2 * slots, 2 * c), BF),
                pltpu.VMEM((2, GROUP, length // 2 * boxes, 2 * slots), BF),
                pltpu.VMEM((2, GROUP * boxes, length * c), BF),
                pltpu.VMEM((wedges, c, p), BF),
                pltpu.VMEM((wedges, p, c), BF),
                pltpu.SemaphoreType.DMA((2, wedges // GROUP)),
            ],
            compiler_params=pltpu.CompilerParams(vmem_limit_bytes=40 << 20),
            name="main",
        )(place, near, far, pick, tcat, lists, pltpu.with_memory_space_constraint(up_ops, pltpu.HBM), pltpu.with_memory_space_constraint(down_ops, pltpu.HBM))
        return out.reshape(boxes, 1, p)

    in_specs = (P("box", "wedge", None), P(), P(), P(), P("box", None), P("box", "wedge", None))
    out_specs = P("box", "wedge", None)
    return jax.shard_map(parts, mesh=mesh, in_specs=in_specs, out_specs=out_specs, check_vma=False)
```

```python
import jax
import jax.numpy as jnp
from jax import lax
from jax.experimental import pallas as pl
from jax.experimental.pallas import tpu as pltpu
from jax.sharding import PartitionSpec as P


BF = jnp.bfloat16
F32 = jnp.float32
NT = (((1,), (1,)), ((), ()))
GROUP = 8
VMEM = pl.BlockSpec(memory_space=pltpu.VMEM)
SMEM = pl.BlockSpec(memory_space=pltpu.SMEM)
HBM = pl.BlockSpec(memory_space=pltpu.HBM)


def pack_kernel(list_ref, out_ref):
    length, boxes = list_ref.shape[1:]
    for k in range(length):
        out_ref[:, k * boxes : (k + 1) * boxes] = list_ref[:, k, :].astype(F32).astype(BF)


def table_kernel(place_ref, table_ref, trans_ref, pick_ref, tcat_ref):
    slots = table_ref.shape[1]
    length, c, _ = trans_ref.shape
    half = pick_ref.shape[1] // 2
    table = table_ref[...]
    owner = table >> 5
    other = (owner & 1) != place_ref[0]
    target = jnp.where(other, half, 0) + ((owner >> 1) << 5) + (table & 31)
    spread = jnp.broadcast_to(target.astype(F32), (slots, slots)).T
    number = lax.broadcasted_iota(jnp.int32, (slots, slots), 1).astype(F32)
    for j in range(2 * half // slots):
        pick_ref[:, j * slots : (j + 1) * slots] = jnp.where(spread == number + float(j * slots), 1.0, 0.0).astype(BF)
    for k in range(length):
        tcat_ref[k * c : (k + 1) * c, :] = trans_ref[k].T


def main_kernel(place_ref, near_ref, far_ref, pick_ref, tcat_ref, *refs):
    list_refs, (up_hbm, down_hbm, out_ref, lists, dens, blocks, sel, wide, held, up, down, sems) = refs[:-12], refs[-12:]
    wedges, c, p = up.shape
    half = near_ref.shape[0]
    slots = pick_ref.shape[0]
    boxes = out_ref.shape[0]
    length = tcat_ref.shape[0] // c
    pieces = len(list_refs)
    here = wedges // pieces
    steps = wedges // GROUP

    def fetch(hbm, ref, kind, piece, skip, count, at):
        group = lax.rem(place_ref[1] + pieces - piece, pieces)
        source = pl.ds(pl.multiple_of(group * here + skip, GROUP), count)
        return pltpu.make_async_copy(hbm.at[source], ref.at[pl.ds(piece * here + skip, count)], sems.at[kind, at])

    ups = [fetch(up_hbm, up, 0, 0, 0, GROUP, 0), fetch(up_hbm, up, 0, 0, GROUP, here - GROUP, 1)]
    ups += [fetch(up_hbm, up, 0, n, 0, here, n + 1) for n in range(1, pieces)]
    downs = [fetch(down_hbm, down, 1, n, 0, here, n) for n in range(pieces)]
    for copy in ups[:2] + downs[:1]:
        copy.start()
    for n in range(1, pieces):
        ups[n + 1].start()
        downs[n].start()

    for n, ref in enumerate(list_refs):
        lists[n * here : (n + 1) * here, :] = ref[...].astype(F32)
    blank = jnp.zeros((GROUP // 2, slots, c), BF)
    for slot in range(2):
        blocks[slot, :, :slots, c:] = blank
        blocks[slot, :, slots:, :c] = blank
    held[1] = jnp.zeros(held.shape[1:], BF)
    number = lax.broadcasted_iota(jnp.int32, (slots, slots), 0).astype(F32)
    chunks = lists.shape[1] // slots

    def rows_of(i):
        return lists[pl.ds(pl.multiple_of(i * GROUP, GROUP), GROUP), :]

    def select(rows, slot, w):
        for j in range(chunks):
            row = jnp.broadcast_to(rows[w : w + 1, j * slots : (j + 1) * slots], (slots, slots))
            hit = jnp.where(row == number, 1.0, 0.0).astype(BF)
            sel[slot, w // 2, j * slots : (j + 1) * slots, w % 2 * slots : (w % 2 + 1) * slots] = hit.T

    def equivalents(i, slot):
        maps = up[pl.ds(pl.multiple_of(i * GROUP, GROUP), GROUP)].reshape(GROUP * c, p)
        value = lax.dot_general(dens[...], maps, NT, preferred_element_type=F32).astype(BF)
        for w in range(GROUP):
            blocks[slot, w // 2, w % 2 * slots : (w % 2 + 1) * slots, w % 2 * c : (w % 2 + 1) * c] = (
                value[:, w * c : (w + 1) * c]
            )

    def gather(slot, pair):
        sources = jnp.dot(sel[slot, pair], blocks[slot, pair], preferred_element_type=F32).astype(BF)
        for k in range(length):
            for d in range(2):
                w = 2 * pair + d
                wide[slot, w * boxes : (w + 1) * boxes, k * c : (k + 1) * c] = (
                    sources[k * boxes : (k + 1) * boxes, d * c : (d + 1) * c]
                )

    def translate(slot):
        local = jnp.dot(wide[slot], tcat_ref[...], preferred_element_type=F32).astype(BF)
        for w in range(GROUP):
            held[slot, :, w * c : (w + 1) * c] = local[w * boxes : (w + 1) * boxes]

    def lower(i, slot, total):
        maps = jnp.concatenate([down[i * GROUP + w] for w in range(GROUP)], 1)
        return total + lax.dot_general(held[slot], maps, NT, preferred_element_type=F32)

    rows = rows_of(0)
    for w in range(GROUP):
        select(rows, 0, w)
    picked = jnp.dot(pick_ref[:, :half], near_ref[...], preferred_element_type=F32)
    picked += jnp.dot(pick_ref[:, half:], far_ref[...], preferred_element_type=F32)
    dens[...] = picked.astype(BF)
    ups[0].wait()
    equivalents(0, 0)

    due = {}
    for n, copy in enumerate(ups[1:]):
        first = GROUP if n == 0 else n * here
        due.setdefault(max(first // GROUP - 1, 0) // 2, []).append(copy)
    for n, copy in enumerate(downs):
        due.setdefault(n * here // GROUP // 2, []).append(copy)

    def step(b, total):
        for at, copies in due.items():

            @pl.when(b == at)
            def _():
                for copy in copies:
                    copy.wait()

        for h in (0, 1):
            now = b * 2 + h
            later = lax.rem(now + 1, steps)
            rows = rows_of(later)
            total = lower(jnp.maximum(now - 1, 0), 1 - h, total)
            for pair in range(GROUP // 2):
                gather(h, pair)
                select(rows, 1 - h, 2 * pair)
                select(rows, 1 - h, 2 * pair + 1)
            equivalents(later, 1 - h)
            translate(h)
        return total

    total = lax.fori_loop(0, steps // 2, step, jnp.zeros((boxes, p), F32))
    out_ref[...] = lower(steps - 1, 1, total).astype(BF)


def solution(mesh):
    x_chips, z_chips, cores = 4, 8, 2
    groups = [[(x * z_chips + z) * cores + c for x in range(x_chips) for z in range(z_chips)] for c in range(cores)]
    swap = [(i, i ^ 1) for i in range(x_chips * z_chips * cores)]

    def parts(densities, up_ops, trans_ops, down_ops, read_table, interaction):
        boxes, _, p = densities.shape
        wedges, c, _ = up_ops.shape
        wedge_here, length = interaction.shape[1:]
        wedge_groups = wedges // wedge_here
        slots = read_table.shape[1]
        chips = len(groups[0])
        half = chips * boxes
        width = length * boxes

        copies = jnp.broadcast_to(densities.reshape(1, boxes, p), (chips, boxes, p))
        near = lax.all_to_all(copies, "box", 0, 0, axis_index_groups=groups)
        near = near.reshape(half, p)

        lists = pl.pallas_call(
            pack_kernel,
            in_specs=[VMEM],
            out_specs=VMEM,
            out_shape=jax.ShapeDtypeStruct((wedge_here, width), BF),
            compiler_params=pltpu.CompilerParams(vmem_limit_bytes=4 << 20),
            name="pack",
        )(interaction.transpose(1, 2, 0))
        spread = [lists]
        for j in range(1, wedge_groups):
            spread.append(lax.ppermute(lists, "wedge", [(i, (i + j) % wedge_groups) for i in range(wedge_groups)]))
        place = jnp.stack([lax.axis_index("box") % cores, lax.axis_index("wedge")])

        pick, tcat = pl.pallas_call(
            table_kernel,
            in_specs=[SMEM, VMEM, VMEM],
            out_specs=[VMEM, VMEM],
            out_shape=[
                jax.ShapeDtypeStruct((slots, 2 * half), BF),
                jax.ShapeDtypeStruct((length * c, c), BF),
            ],
            compiler_params=pltpu.CompilerParams(vmem_limit_bytes=4 << 20),
            name="tables",
        )(place, read_table, trans_ops)

        far = lax.ppermute(near, "box", swap)

        out = pl.pallas_call(
            main_kernel,
            in_specs=[SMEM] + [VMEM] * (4 + wedge_groups) + [HBM, HBM],
            out_specs=VMEM,
            out_shape=jax.ShapeDtypeStruct((boxes, p), BF),
            scratch_shapes=[
                pltpu.VMEM((wedges, width), F32),
                pltpu.VMEM((slots, p), BF),
                pltpu.VMEM((2, GROUP // 2, 2 * slots, 2 * c), BF),
                pltpu.VMEM((2, GROUP // 2, width, 2 * slots), BF),
                pltpu.VMEM((2, GROUP * boxes, length * c), BF),
                pltpu.VMEM((2, boxes, GROUP * c), BF),
                pltpu.VMEM((wedges, c, p), BF),
                pltpu.VMEM((wedges, p, c), BF),
                pltpu.SemaphoreType.DMA((2, wedge_groups + 1)),
            ],
            compiler_params=pltpu.CompilerParams(vmem_limit_bytes=40 << 20),
            name="main",
        )(
            place, near, far, pick, tcat, *spread,
            pltpu.with_memory_space_constraint(up_ops, pltpu.HBM),
            pltpu.with_memory_space_constraint(down_ops, pltpu.HBM),
        )
        return out.reshape(boxes, 1, p)

    in_specs = (P("box", "wedge", None), P(), P(), P(), P("box", None), P("box", "wedge", None))
    out_specs = P("box", "wedge", None)
    return jax.shard_map(parts, mesh=mesh, in_specs=in_specs, out_specs=out_specs, check_vma=False)
```

```python
import jax
import jax.numpy as jnp
from jax import lax
from jax.experimental import pallas as pl
from jax.experimental.pallas import tpu as pltpu
from jax.sharding import PartitionSpec as P


BF = jnp.bfloat16
F32 = jnp.float32
NT = (((1,), (1,)), ((), ()))
GROUP = 8
VMEM = pl.BlockSpec(memory_space=pltpu.VMEM)
SMEM = pl.BlockSpec(memory_space=pltpu.SMEM)
HBM = pl.BlockSpec(memory_space=pltpu.HBM)


def pack_kernel(list_ref, out_ref):
    length, boxes = list_ref.shape[1:]
    for k in range(length):
        out_ref[:, k * boxes : (k + 1) * boxes] = list_ref[:, k, :].astype(F32).astype(BF)


def table_kernel(place_ref, table_ref, trans_ref, pick_ref, tcat_ref):
    slots = table_ref.shape[1]
    length, c, _ = trans_ref.shape
    half = pick_ref.shape[1] // 2
    table = table_ref[...]
    owner = table >> 5
    other = (owner & 1) != place_ref[0]
    target = jnp.where(other, half, 0) + ((owner >> 1) << 5) + (table & 31)
    spread = jnp.broadcast_to(target.astype(F32), (slots, slots)).T
    number = lax.broadcasted_iota(jnp.int32, (slots, slots), 1).astype(F32)
    for j in range(2 * half // slots):
        pick_ref[:, j * slots : (j + 1) * slots] = jnp.where(spread == number + float(j * slots), 1.0, 0.0).astype(BF)
    for k in range(length):
        tcat_ref[k * c : (k + 1) * c, :] = trans_ref[k].T


def main_kernel(place_ref, near_ref, far_ref, pick_ref, tcat_ref, *refs):
    list_refs, (up_hbm, down_hbm, out_ref, lists, dens, blocks, sel, wide, held, up, down, sems) = refs[:-12], refs[-12:]
    wedges, c, p = up.shape
    half = near_ref.shape[0]
    slots = pick_ref.shape[0]
    boxes = out_ref.shape[0]
    length = tcat_ref.shape[0] // c
    pieces = len(list_refs)
    here = wedges // pieces
    steps = wedges // GROUP

    def fetch(hbm, ref, kind, piece, skip, count, at):
        group = lax.rem(place_ref[1] + pieces - piece, pieces)
        source = pl.ds(pl.multiple_of(group * here + skip, GROUP), count)
        return pltpu.make_async_copy(hbm.at[source], ref.at[pl.ds(piece * here + skip, count)], sems.at[kind, at])

    ups = [fetch(up_hbm, up, 0, 0, 0, GROUP, 0), fetch(up_hbm, up, 0, 0, GROUP, here - GROUP, 1)]
    ups += [fetch(up_hbm, up, 0, n, 0, here, n + 1) for n in range(1, pieces)]
    downs = [fetch(down_hbm, down, 1, n, 0, here, n) for n in range(pieces)]
    for copy in ups[:2] + downs[:1]:
        copy.start()
    for n in range(1, pieces):
        ups[n + 1].start()
        downs[n].start()

    for n, ref in enumerate(list_refs):
        lists[n * here : (n + 1) * here, :] = ref[...].astype(F32)
    held[1] = jnp.zeros(held.shape[1:], BF)
    number = lax.broadcasted_iota(jnp.int32, (slots, slots), 0).astype(F32)
    chunks = lists.shape[1] // slots

    def rows_of(i):
        return lists[pl.ds(pl.multiple_of(i * GROUP, GROUP), GROUP), :]

    def select(rows, slot, w):
        for j in range(chunks):
            row = jnp.broadcast_to(rows[w : w + 1, j * slots : (j + 1) * slots], (slots, slots))
            hit = jnp.where(row == number, 1.0, 0.0).astype(BF)
            sel[slot, w, j * slots : (j + 1) * slots, :] = hit.T

    def equivalents(i, slot):
        maps = up[pl.ds(pl.multiple_of(i * GROUP, GROUP), GROUP)].reshape(GROUP * c, p)
        value = lax.dot_general(dens[...], maps, NT, preferred_element_type=F32).astype(BF)
        for w in range(GROUP):
            blocks[slot, w] = value[:, w * c : (w + 1) * c]

    def gather(slot, w):
        sources = jnp.dot(sel[slot, w], blocks[slot, w], preferred_element_type=F32).astype(BF)
        for k in range(length):
            wide[slot, w * boxes : (w + 1) * boxes, k * c : (k + 1) * c] = sources[k * boxes : (k + 1) * boxes]

    def translate(slot):
        local = jnp.dot(wide[slot], tcat_ref[...], preferred_element_type=F32).astype(BF)
        for w in range(GROUP):
            held[slot, :, w * c : (w + 1) * c] = local[w * boxes : (w + 1) * boxes]

    def lower(i, slot, total):
        maps = jnp.concatenate([down[i * GROUP + w] for w in range(GROUP)], 1)
        return total + lax.dot_general(held[slot], maps, NT, preferred_element_type=F32)

    rows = rows_of(0)
    for w in range(GROUP):
        select(rows, 0, w)
    picked = jnp.dot(pick_ref[:, :half], near_ref[...], preferred_element_type=F32)
    picked += jnp.dot(pick_ref[:, half:], far_ref[...], preferred_element_type=F32)
    dens[...] = picked.astype(BF)
    ups[0].wait()
    equivalents(0, 0)

    due = {}
    for n, copy in enumerate(ups[1:]):
        first = GROUP if n == 0 else n * here
        due.setdefault(max(first // GROUP - 1, 0) // 2, []).append(copy)
    for n, copy in enumerate(downs):
        due.setdefault(n * here // GROUP // 2, []).append(copy)

    def step(b, total):
        for at, copies in due.items():

            @pl.when(b == at)
            def _():
                for copy in copies:
                    copy.wait()

        for h in (0, 1):
            now = b * 2 + h
            later = lax.rem(now + 1, steps)
            rows = rows_of(later)
            total = lower(jnp.maximum(now - 1, 0), 1 - h, total)
            for w in range(GROUP):
                gather(h, w)
                select(rows, 1 - h, w)
            equivalents(later, 1 - h)
            translate(h)
        return total

    total = lax.fori_loop(0, steps // 2, step, jnp.zeros((boxes, p), F32))
    out_ref[...] = lower(steps - 1, 1, total).astype(BF)


def solution(mesh):
    x_chips, z_chips, cores = 4, 8, 2
    groups = [[(x * z_chips + z) * cores + c for x in range(x_chips) for z in range(z_chips)] for c in range(cores)]
    swap = [(i, i ^ 1) for i in range(x_chips * z_chips * cores)]

    def parts(densities, up_ops, trans_ops, down_ops, read_table, interaction):
        boxes, _, p = densities.shape
        wedges, c, _ = up_ops.shape
        wedge_here, length = interaction.shape[1:]
        wedge_groups = wedges // wedge_here
        slots = read_table.shape[1]
        chips = len(groups[0])
        half = chips * boxes
        width = length * boxes

        copies = jnp.broadcast_to(densities.reshape(1, boxes, p), (chips, boxes, p))
        near = lax.all_to_all(copies, "box", 0, 0, axis_index_groups=groups)
        near = near.reshape(half, p)

        lists = pl.pallas_call(
            pack_kernel,
            in_specs=[VMEM],
            out_specs=VMEM,
            out_shape=jax.ShapeDtypeStruct((wedge_here, width), BF),
            compiler_params=pltpu.CompilerParams(vmem_limit_bytes=4 << 20),
            name="pack",
        )(interaction.transpose(1, 2, 0))
        spread = [lists]
        for j in range(1, wedge_groups):
            spread.append(lax.ppermute(lists, "wedge", [(i, (i + j) % wedge_groups) for i in range(wedge_groups)]))
        place = jnp.stack([lax.axis_index("box") % cores, lax.axis_index("wedge")])

        pick, tcat = pl.pallas_call(
            table_kernel,
            in_specs=[SMEM, VMEM, VMEM],
            out_specs=[VMEM, VMEM],
            out_shape=[
                jax.ShapeDtypeStruct((slots, 2 * half), BF),
                jax.ShapeDtypeStruct((length * c, c), BF),
            ],
            compiler_params=pltpu.CompilerParams(vmem_limit_bytes=4 << 20),
            name="tables",
        )(place, read_table, trans_ops)

        far = lax.ppermute(near, "box", swap)

        out = pl.pallas_call(
            main_kernel,
            in_specs=[SMEM] + [VMEM] * (4 + wedge_groups) + [HBM, HBM],
            out_specs=VMEM,
            out_shape=jax.ShapeDtypeStruct((boxes, p), BF),
            scratch_shapes=[
                pltpu.VMEM((wedges, width), F32),
                pltpu.VMEM((slots, p), BF),
                pltpu.VMEM((2, GROUP, slots, c), BF),
                pltpu.VMEM((2, GROUP, width, slots), BF),
                pltpu.VMEM((2, GROUP * boxes, length * c), BF),
                pltpu.VMEM((2, boxes, GROUP * c), BF),
                pltpu.VMEM((wedges, c, p), BF),
                pltpu.VMEM((wedges, p, c), BF),
                pltpu.SemaphoreType.DMA((2, wedge_groups + 1)),
            ],
            compiler_params=pltpu.CompilerParams(vmem_limit_bytes=40 << 20),
            name="main",
        )(
            place, near, far, pick, tcat, *spread,
            pltpu.with_memory_space_constraint(up_ops, pltpu.HBM),
            pltpu.with_memory_space_constraint(down_ops, pltpu.HBM),
        )
        return out.reshape(boxes, 1, p)

    in_specs = (P("box", "wedge", None), P(), P(), P(), P("box", None), P("box", "wedge", None))
    out_specs = P("box", "wedge", None)
    return jax.shard_map(parts, mesh=mesh, in_specs=in_specs, out_specs=out_specs, check_vma=False)
```
